256 devices in a mesh: lat: 16 (over x, y), mem: 16 (over z, core).
Axes of the slice: x: 4, y: 4, z: 8, core: 2. Of those that a mesh axis runs over, the one named last changes fastest.
Arguments:
- latent_field: bfloat16 [32, 16, 720, 256], P('mem', 'lat'), may hold values from -36 to 36
- norm_multipliers: float32 [2, 256], replicated, may hold values from 0.1 to 1.9
- kernel_coefficients: bfloat16 [2, 2304, 256], replicated, may hold values from -0.125 to 0.125
- expansion_matrix: bfloat16 [2, 256, 1024], replicated, may hold values from -0.375 to 0.375
- contraction_matrix: bfloat16 [2, 1024, 256], replicated, may hold values from -0.1875 to 0.1875
- obs_cell: int32 [16384], P('lat'), may hold values from 0 to 719
- obs_chan: int32 [16384], P('lat'), may hold values from 0 to 255
- obs_value: float32 [16384], P('lat'), may hold values from -16 to 16
- obs_var: float32 [16384], P('lat'), may hold values from 34.1333333 to 409.6
Outputs:
- posterior_latent: bfloat16 [32, 16, 720, 256], P('mem', 'lat')
The draws below stay inside these ranges and needn't reach their ends.
Inputs may be any that keep to these rules, and one draw needn't show every extreme that they name: Observation i lies in latitude rows (i // 1024) * 1 onward; obs_cell[i] counts the cells of those 1 row row by row over 720 longitudes.
All inputs are finite; a program needn't handle non-finite values.
Results may differ from the reference program's by a relative error of at most 0.015.
Values may be sent and summed in bfloat16 or wider, within the bound.
No kernel may reach another device: no remote copies, remote signals or barrier semaphores. Data moves between devices by JAX's collectives and lax.ppermute only.
A program may use at most 192 MiB of HBM per device.

```python
import math
import jax
import jax.numpy as jnp
from jax import lax

C = 256
HID = 1024
LON = 720
LAT_DEV = 1
OBS_DEV = 1024
BLOCKS = 2
NS_ITERS = 6
K = 32
NLAT = 16
NOBS = 16384


def draw_latent_field(key, part):
    noise_key, chan_key, cell_key = jax.random.split(jax.random.fold_in(key, 7), 3)
    full_shape = (K, NLAT, LON, C)
    base = jnp.clip(jax.random.normal(noise_key, full_shape, jnp.float32), -4.0, 4.0)
    chan_scale = jnp.exp(jax.random.uniform(chan_key, (C,), jnp.float32, math.log(0.3), math.log(3.0)))
    cell_scale = jnp.exp(jax.random.uniform(cell_key, (K, NLAT, LON, 1), jnp.float32, math.log(0.3), math.log(3.0)))
    return (base * chan_scale * cell_scale).astype(jnp.bfloat16)


def draw_obs_var(key, part):
    base_key = jax.random.fold_in(key, 13)
    slab_count = NOBS // OBS_DEV
    position = (jnp.arange(NOBS) // OBS_DEV).astype(jnp.float32)
    ramp_value = position / max(slab_count - 1, 1)
    lowest = NOBS / 160.0
    highest = NOBS / 40.0
    base = jnp.exp(jax.random.uniform(base_key, (NOBS,), jnp.float32, math.log(lowest), math.log(highest)))
    return base * jnp.exp(-math.log(3.0) * ramp_value)


def place_ends(values, key, least, largest):
    extent = values.shape
    spot = [jax.random.randint(jax.random.fold_in(key, axis), (), 0, extent[axis]) for axis in range(len(extent))]
    values = values.at[tuple(spot)].set(least)
    longest = extent.index(max(extent))
    spot[longest] = (spot[longest] + 1) % extent[longest]
    return values.at[tuple(spot)].set(largest)


def block_scale(key, dims, cuts, low, top_value):
    def one(dim, shards_of):
        heights = jax.random.uniform(jax.random.fold_in(jax.random.fold_in(key, 6), dim), (shards_of,), jnp.float32, low / len(cuts), top_value / len(cuts))
        return jnp.repeat(jnp.exp(heights), dims[dim] // shards_of).reshape((-1,) + (1,) * (len(dims) - dim - 1))

    level = one(*cuts[0])
    for cut in cuts[1:]:
        level = level * one(*cut)
    return level


def gaussian(stream_key, shape, deviation, limit, cuts=(), kind=jnp.bfloat16):
    values = deviation * jax.random.normal(stream_key, shape, jnp.float32)
    if cuts:
        values = values * block_scale(stream_key, shape, cuts, -0.22, 0.18)
    return jnp.clip(values, -limit, limit).astype(kind)


def setup_inputs(seed: int = 0) -> dict:
    keys = jax.random.split(jax.random.key(seed), 10)
    return {
        "latent_field": draw_latent_field(jax.random.fold_in(keys[9], 71), 0),
        "norm_multipliers": jnp.clip(1.0 + 0.18 * jax.random.normal(keys[1], (BLOCKS, C), jnp.float32), 0.1, 1.9),
        "kernel_coefficients": gaussian(keys[2], (BLOCKS, 9 * C, C), (9 * C) ** -0.5, 0.125),
        "expansion_matrix": gaussian(keys[3], (BLOCKS, C, HID), C ** -0.5, 0.375),
        "contraction_matrix": gaussian(keys[4], (BLOCKS, HID, C), HID ** -0.5, 0.1875),
        "obs_cell": place_ends(jax.random.randint(keys[5], (NOBS,), 0, LAT_DEV * LON), jax.random.fold_in(keys[5], 1), 0, (LAT_DEV * LON) - 1).astype(jnp.int32),
        "obs_chan": place_ends(jax.random.randint(keys[6], (NOBS,), 0, C), jax.random.fold_in(keys[6], 1), 0, C - 1).astype(jnp.int32),
        "obs_value": gaussian(keys[7], (NOBS,), 4.0, 16.0, ((0, 16),), jnp.float32),
        "obs_var": draw_obs_var(jax.random.fold_in(keys[9], 71), 0),
    }


def normed(fields, gain):
    wide = fields.astype(jnp.float32)
    factor = lax.rsqrt(lax.optimization_barrier(jnp.mean(wide * wide, axis=-1, keepdims=True)) + 1e-06)
    return (wide * factor * gain).astype(jnp.bfloat16)

def columns(padded, height):
    pieces = []
    for lat_shift in range(3):
        lat_band = padded[:, lat_shift:lat_shift + height]
        for lon_shift in (-1, 0, 1):
            pieces.append(jnp.roll(lat_band, -lon_shift, axis=2))
    return jnp.concatenate(pieces, axis=-1)

def mix_layer(fields, padded, conv_mat, up_mat, down_mat):
    stacked = columns(padded, fields.shape[1])
    flat_cols = stacked.reshape(-1, stacked.shape[-1])
    conv_out = jnp.dot(flat_cols, conv_mat, preferred_element_type=jnp.float32).astype(jnp.bfloat16)
    hidden = jax.nn.gelu(jnp.dot(conv_out, up_mat, preferred_element_type=jnp.float32)).astype(jnp.bfloat16)
    branch = jnp.dot(hidden, down_mat, preferred_element_type=jnp.float32)
    return (fields.astype(jnp.float32) + branch.reshape(fields.shape)).astype(jnp.bfloat16)

def gram_terms(measured_entries, obs_value, obs_var):
    centre = lax.optimization_barrier(jnp.mean(measured_entries, axis=0))
    anomaly = measured_entries - centre
    scaled = anomaly / obs_var
    gram_part = jnp.dot(scaled, anomaly.T, precision=lax.Precision.HIGHEST)
    drive_part = jnp.dot(scaled, obs_value - centre, precision=lax.Precision.HIGHEST)
    return (gram_part, drive_part)

def transform(gram_sum, drive_sum):
    realization_latents = gram_sum.shape[0]
    identity = jnp.eye(realization_latents, dtype=jnp.float32)
    spread = float(realization_latents - 1)
    system = spread * identity + gram_sum
    bound_value = spread + jnp.trace(gram_sum)
    iterate = system / bound_value
    inv_root = identity
    for sweep in range(NS_ITERS):
        step_mat = 1.5 * identity - 0.5 * jnp.dot(inv_root, iterate, precision=lax.Precision.HIGHEST)
        iterate = jnp.dot(iterate, step_mat, precision=lax.Precision.HIGHEST)
        inv_root = jnp.dot(step_mat, inv_root, precision=lax.Precision.HIGHEST)
    inv_sqrt = inv_root / jnp.sqrt(bound_value)
    mean_shift = jnp.dot(inv_sqrt, jnp.dot(inv_sqrt, drive_sum, precision=lax.Precision.HIGHEST), precision=lax.Precision.HIGHEST)
    weights = math.sqrt(spread) * inv_sqrt + mean_shift[:, None]
    totals = lax.optimization_barrier(jnp.sum(weights, axis=0))
    return (weights + (1.0 - totals)[None, :] / realization_latents).astype(jnp.bfloat16)

def propagate_realization(realization_latent, norm_multipliers, kernel_coefficients, expansion_matrix, contraction_matrix):
    fields = realization_latent[None]
    for layer_index in range(BLOCKS):
        unit = normed(fields, norm_multipliers[layer_index])
        padded = jnp.pad(unit, ((0, 0), (1, 1), (0, 0), (0, 0)))
        fields = mix_layer(fields, padded, kernel_coefficients[layer_index], expansion_matrix[layer_index], contraction_matrix[layer_index])
    return fields[0]

def reference(latent_field, norm_multipliers, kernel_coefficients, expansion_matrix, contraction_matrix, obs_cell, obs_chan, obs_value, obs_var):
    prior_latent = lax.map(lambda realization_latent: propagate_realization(realization_latent, norm_multipliers, kernel_coefficients, expansion_matrix, contraction_matrix), latent_field)
    realization_latents = prior_latent.shape[0]
    slab_index = jnp.arange(NOBS, dtype=jnp.int32) // OBS_DEV
    linear_position = ((slab_index * (LAT_DEV * LON) + obs_cell) * C + obs_chan).astype(jnp.int32)
    raveled_prior = prior_latent.reshape(realization_latents, -1)
    measured_entries = jnp.take(raveled_prior, linear_position, axis=1).astype(jnp.float32)
    gram_sum, drive_sum = gram_terms(measured_entries, obs_value, obs_var)
    square_array = transform(gram_sum, drive_sum)
    posterior_latent = lax.map(lambda grid_column_entry: jnp.dot(grid_column_entry, raveled_prior, preferred_element_type=jnp.float32).astype(jnp.bfloat16), square_array.T)
    return posterior_latent.reshape(prior_latent.shape)
```

```python
import functools
import math

import jax
import jax.numpy as jnp
from jax import lax
from jax.experimental import pallas as pl
from jax.experimental.pallas import tpu as pltpu
from jax.sharding import PartitionSpec as P

BLOCKS = 2
NS_ITERS = 6
F32 = jnp.float32
BF16 = jnp.bfloat16
HIGHEST = lax.Precision.HIGHEST
VMEM = pl.BlockSpec(memory_space=pltpu.VMEM)
SMEM = pl.BlockSpec(memory_space=pltpu.SMEM)
HBM = pl.BlockSpec(memory_space=pltpu.HBM)


def call(body, out_shape, args, specs=None, out_specs=None, scratch=(), mib=24, flops=0, nbytes=0, **kw):
    return pl.pallas_call(
        body,
        out_shape=out_shape,
        in_specs=specs or [VMEM] * len(args),
        out_specs=out_specs if out_specs is not None else jax.tree.map(lambda _: VMEM, out_shape),
        scratch_shapes=list(scratch),
        compiler_params=pltpu.CompilerParams(vmem_limit_bytes=mib << 20),
        cost_estimate=pl.CostEstimate(flops=flops, bytes_accessed=nbytes, transcendentals=0),
        **kw,
    )(*args)


def shaped(shape, dtype):
    return jax.ShapeDtypeStruct(shape, dtype)


def normed(wide, gain):
    factor = lax.rsqrt(jnp.mean(wide * wide, axis=-1, keepdims=True) + 1e-06)
    return (wide * factor * gain).astype(BF16)


def first_norm(x_ref, gain_ref, *unit_refs):
    for m, ref in enumerate(unit_refs):
        ref[...] = normed(x_ref[m, 0].astype(F32), gain_ref[0:1, :])


def load_body(*refs):
    sems, refs = refs[-1], refs[:-1]
    count = len(refs) // 2
    copies = []
    for ref, into in zip(refs[:count], refs[count:]):
        rows = ref.shape[1] // 4
        for b in range(ref.shape[0]):
            for i in range(4):
                part = pl.ds(i * rows, rows)
                copies.append(
                    pltpu.make_async_copy(ref.at[b, part], into.at[b, part], sems.at[len(copies)])
                )
    for copy in copies:
        copy.start()
    for copy in copies:
        copy.wait()


def block_body(b, member, odd_ref, x_ref, near_ref, mid_ref, far_ref, conv_ref, up_ref, down_ref, *rest):
    last = b == BLOCKS - 1
    *rest, mixed = rest
    if last and member == 0:
        cell_ref, chan_ref, out_ref, seen_ref, fields_ref = rest
    elif last:
        cell_ref, chan_ref, seen_ref, out_ref, fields_ref = rest
    elif member == 0:
        gain_ref, later_ref, fields_ref, pair_ref = rest
        unit_ref = pair_ref.at[0]
        pair_ref[1] = later_ref[...]
    else:
        gain_ref, fields_ref, unit_ref = rest
    lon, ch = x_ref.shape
    rows = jnp.concatenate([near_ref[...], mid_ref[...], far_ref[...]], axis=1)
    lines = (2 - 2 * odd_ref[0], 1, 2 * odd_ref[0])
    parts = []
    for q in range(3):
        taps = [
            conv_ref[b, pl.ds(pl.multiple_of((p * 3 + q) * ch, ch), ch), :] for p in lines
        ]
        parts.append(jnp.dot(rows, jnp.concatenate(taps, axis=0), preferred_element_type=F32))
    mixed[...] = (
        pltpu.roll(parts[0], 1, 0) + parts[1] + pltpu.roll(parts[2], lon - 1, 0)
    ).astype(BF16)
    step = 144
    for start in range(0, lon, step):
        part = pl.ds(start, step)
        hidden = jax.nn.gelu(jnp.dot(mixed[part, :], up_ref[b], preferred_element_type=F32))
        branch = jnp.dot(hidden.astype(BF16), down_ref[b], preferred_element_type=F32)
        fields = (x_ref[part, :].astype(F32) + branch).astype(BF16)
        fields_ref[part, :] = fields
        if not last:
            unit_ref[part, :] = normed(fields.astype(F32), gain_ref[b + 1 : b + 2, :])
    if last:
        owners = out_ref.shape[0]
        cells = fields_ref.shape[0] // owners
        count = cell_ref.shape[1]
        at_cell = lax.broadcasted_iota(jnp.int32, (lon, count), 0) == cell_ref[...]
        pick = jnp.where(at_cell, 1.0, 0.0).astype(BF16)
        column = lax.dot_general(
            fields_ref[:lon, :], pick, (((0,), (0,)), ((), ())), preferred_element_type=F32
        )
        at_chan = lax.broadcasted_iota(jnp.int32, (ch, count), 0) == chan_ref[...]
        seen = jnp.sum(jnp.where(at_chan, column, 0.0), axis=0, keepdims=True)
        seen = [seen[:, i : i + ch] for i in range(0, count, ch)]
        fields_ref[lon:, :] = jnp.zeros((owners * cells - lon, ch), BF16)
        for i in range(owners):
            out_ref[i, :cells, :] = fields_ref[i * cells : (i + 1) * cells, :]
        if member == 0:
            seen_ref[...] = jnp.concatenate(seen, axis=0)
        else:
            both = jnp.concatenate([seen_ref[...], *seen], axis=0).astype(BF16)
            for i in range(owners):
                out_ref[i, cells:, :] = both


def gram_body(seen_ref, value_ref, var_ref, out_ref):
    owners, _, ch = seen_ref.shape
    lines = value_ref.shape[0]
    seen = seen_ref[...].astype(F32)
    members = 2 * owners
    twice = lambda ref: jnp.concatenate([ref[...], ref[...]], axis=0)
    half = jnp.sum(seen, axis=0)
    centre = (half + pltpu.roll(half, lines, 0)) / members
    anomaly = seen - centre[None]
    scaled = anomaly / twice(var_ref)[None]
    rows = owners * 8
    right = jnp.concatenate([anomaly.reshape(rows, ch), twice(value_ref) - centre], axis=0)
    terms = lax.dot_general(
        scaled.reshape(rows, ch),
        right,
        (((1,), (1,)), ((), ())),
        precision=HIGHEST,
        preferred_element_type=F32,
    )
    row = lax.broadcasted_iota(jnp.int32, terms.shape, 0)
    col = lax.broadcasted_iota(jnp.int32, terms.shape, 1)
    terms = jnp.where((row % lines == col % lines) & (col < rows + lines), terms, 0.0)
    dot = functools.partial(jnp.dot, precision=HIGHEST, preferred_element_type=F32)
    left = jnp.where(
        lax.broadcasted_iota(jnp.int32, (members, rows), 0)
        == lax.broadcasted_iota(jnp.int32, (members, rows), 1) // lines,
        1.0,
        0.0,
    )
    gather = jnp.where(
        lax.broadcasted_iota(jnp.int32, (rows + 8, 128), 0) // lines
        == lax.broadcasted_iota(jnp.int32, (rows + 8, 128), 1),
        1.0,
        0.0,
    )
    out_ref[...] = dot(dot(left, terms), gather)


def transform_body(a_ref, b_ref, c_ref, d_ref, out_ref):
    total = (a_ref[...] + b_ref[...]) + (c_ref[...] + d_ref[...])
    members = total.shape[0]
    dot = functools.partial(jnp.dot, precision=HIGHEST, preferred_element_type=F32)
    row = lax.broadcasted_iota(jnp.int32, (members, members), 0)
    col = lax.broadcasted_iota(jnp.int32, (members, members), 1)
    identity = jnp.where(row == col, 1.0, 0.0)
    spread = float(members - 1)
    gram = total[:, :members]
    bound_value = spread + jnp.sum(gram * identity)
    iterate = (spread * identity + gram) / bound_value
    inv_root = identity
    for _ in range(NS_ITERS):
        step_mat = 1.5 * identity - 0.5 * dot(inv_root, iterate)
        iterate = dot(iterate, step_mat)
        inv_root = dot(step_mat, inv_root)
    inv_sqrt = inv_root / jnp.sqrt(bound_value)
    shift = dot(inv_sqrt, dot(inv_sqrt, total))[:, members : members + 1]
    weights = math.sqrt(spread) * inv_sqrt + shift
    totals = jnp.sum(weights, axis=0, keepdims=True)
    out_ref[...] = (weights + (1.0 - totals) / members).astype(BF16)


def combine_body(weight_ref, even_ref, odd_ref, out_ref):
    members = weight_ref.shape[0]
    owners = even_ref.shape[0]
    cells = out_ref.shape[1]
    group = 16
    rows = members * group
    spread = jnp.where(
        lax.broadcasted_iota(jnp.int32, (rows, members), 0) // group
        == lax.broadcasted_iota(jnp.int32, (rows, members), 1),
        1.0,
        0.0,
    ).astype(BF16)
    tall = lax.dot_general(
        spread, weight_ref[...], (((1,), (1,)), ((), ())), preferred_element_type=F32
    ).astype(BF16)
    wide = lax.dot_general(tall, spread, (((1,), (1,)), ((), ())), preferred_element_type=F32)
    same = (
        lax.broadcasted_iota(jnp.int32, (rows, rows), 0) % group
        == lax.broadcasted_iota(jnp.int32, (rows, rows), 1) % group
    )
    kron = jnp.where(same, wide, 0.0).astype(BF16)
    for start in range(0, cells, group):
        part = pl.ds(start, group)
        data = jnp.concatenate(
            [ref[i, part, :] for i in range(owners) for ref in (even_ref, odd_ref)], axis=0
        )
        sums = jnp.dot(kron, data, preferred_element_type=F32).astype(BF16)
        for i in range(members):
            out_ref[i, part, :] = sums[i * group : (i + 1) * group, :]


def place_body(in_ref, out_ref):
    lon = out_ref.shape[2]
    cells = in_ref.shape[2]
    for i in range(lon // cells):
        for m in range(out_ref.shape[0]):
            out_ref[m, 0, i * cells : (i + 1) * cells, :] = in_ref[i, m]


def body(latent, gains, conv, up, down, obs_cell, obs_chan, obs_value, obs_var):
    members, _, lon, ch = latent.shape
    count = obs_cell.shape[0]
    lat = lax.axis_size("lat")
    mem = lax.axis_size("mem")
    cell, chan = (v.reshape(1, count) for v in (obs_cell, obs_chan))
    value, var = (v.reshape(count // ch, ch) for v in (obs_value, obs_var))
    held = [pltpu.VMEM((lon, ch), BF16)]
    odd_row = (lax.axis_index("lat") % 2).reshape(1)
    work = 2 * lon * (9 * ch * ch + 2 * ch * up.shape[2])
    row = shaped((lon, ch), BF16)
    pair = shaped((members, lon, ch), BF16)
    cells = -(-lon // (mem * 16)) * 16

    def slot(m):
        return pl.BlockSpec((None, lon, ch), lambda i: (m, 0, 0))

    def halo(unit):
        pairs = [[(i, i + 1) for i in range(start, lat - 1, 2)] for start in (0, 1)]
        return [lax.ppermute(unit, "lat", p + [(j, i) for i, j in p]) for p in pairs]

    def block(b, m, x, before, mid, after, extra, outs, x_spec, halo_spec, scratch=()):
        return call(
            functools.partial(block_body, b, m),
            outs,
            (odd_row, x, before, mid, after, *held_weights, *extra),
            [SMEM, x_spec, halo_spec, halo_spec, halo_spec] + [VMEM] * (3 + len(extra)),
            grid=(1,),
            scratch=[*scratch, *held],
            mib=32,
            flops=work,
            nbytes=8 * lon * ch * 2,
        )

    def latent_spec(m):
        return pl.BlockSpec((None, None, lon, ch), lambda i: (m, 0, 0, 0))

    first, second = call(first_norm, (row, row), (latent, gains), nbytes=8 * lon * ch)
    before, after = halo(first)
    weights = (conv, up, down)
    held_weights = call(
        load_body,
        tuple(shaped(w.shape, BF16) for w in weights),
        weights,
        [HBM] * 3,
        scratch=[pltpu.SemaphoreType.DMA((24,))],
        mib=32,
        nbytes=sum(2 * w.size for w in weights),
    )
    fields_a, units = block(
        0, 0, latent, before, first, after, (gains, second), (row, pair), latent_spec(0), VMEM
    )
    before, after = halo(units)
    fields_b, last = block(
        0, 1, latent, before, units, after, (gains,), (row, row), latent_spec(1), slot(1)
    )
    plain = shaped((mem, cells, ch), BF16)
    with_seen = shaped((mem, cells + 8, ch), BF16)
    store = [pltpu.VMEM((mem * cells, ch), BF16)]
    fields_a, last = lax.optimization_barrier((fields_a, last))
    last_before, last_after = halo(last)
    even, seen = block(
        1,
        0,
        fields_a,
        before,
        units,
        after,
        (cell, chan),
        (plain, shaped((count // ch, ch), F32)),
        VMEM,
        slot(0),
        store,
    )
    even = lax.all_to_all(even, "mem", 0, 0, tiled=True)
    odd = block(
        1, 1, fields_b, last_before, last, last_after, (cell, chan, seen), with_seen, VMEM, VMEM, store
    )
    odd = lax.all_to_all(odd, "mem", 0, 0, tiled=True)

    def swap(v, axis, steps):
        size = {"lat": lat, "mem": mem}[axis]
        return [v] + [lax.ppermute(v, axis, [(i, i ^ s) for i in range(size)]) for s in steps]

    square = shaped((members * mem, 128), F32)
    terms = call(
        gram_body,
        square,
        (odd, value, var),
        [pl.BlockSpec((mem, 8, ch), lambda i: (0, cells // 8, 0)), VMEM, VMEM],
        grid=(1,),
    )
    terms = sum(swap(terms, "lat", (1, 2, 3)))
    sums = swap(terms, "lat", (4, 8, 12))
    weights = call(transform_body, shaped((members * mem, members * mem), BF16), sums)
    mixed = call(combine_body, shaped((members * mem, cells, ch), BF16), (weights, even, odd))
    mixed = lax.all_to_all(mixed.reshape(mem, members, cells, ch), "mem", 0, 0, tiled=True)
    return call(place_body, shaped(latent.shape, BF16), (mixed,))


def solution(mesh):
    in_specs = (
        P("mem", "lat", None, None),
        P(),
        P(),
        P(),
        P(),
        P("lat"),
        P("lat"),
        P("lat"),
        P("lat"),
    )
    out_specs = P("mem", "lat", None, None)
    return jax.shard_map(body, mesh=mesh, in_specs=in_specs, out_specs=out_specs, check_vma=False)
```

```python
import functools
import math

import jax
import jax.numpy as jnp
from jax import lax
from jax.experimental import pallas as pl
from jax.experimental.pallas import tpu as pltpu
from jax.sharding import PartitionSpec as P

BLOCKS = 2
NS_ITERS = 6
F32 = jnp.float32
BF16 = jnp.bfloat16
HIGHEST = lax.Precision.HIGHEST
VMEM = pl.BlockSpec(memory_space=pltpu.VMEM)
SMEM = pl.BlockSpec(memory_space=pltpu.SMEM)
HBM = pl.BlockSpec(memory_space=pltpu.HBM)


def call(body, out_shape, args, specs=None, out_specs=None, scratch=(), mib=24, flops=0, nbytes=0, **kw):
    return pl.pallas_call(
        body,
        out_shape=out_shape,
        in_specs=specs or [VMEM] * len(args),
        out_specs=out_specs if out_specs is not None else jax.tree.map(lambda _: VMEM, out_shape),
        scratch_shapes=list(scratch),
        compiler_params=pltpu.CompilerParams(vmem_limit_bytes=mib << 20),
        cost_estimate=pl.CostEstimate(flops=flops, bytes_accessed=nbytes, transcendentals=0),
        **kw,
    )(*args)


def shaped(shape, dtype):
    return jax.ShapeDtypeStruct(shape, dtype)


def normed(wide, gain):
    factor = lax.rsqrt(jnp.mean(wide * wide, axis=-1, keepdims=True) + 1e-06)
    return (wide * factor * gain).astype(BF16)


def first_norm(x_ref, gain_ref, *unit_refs):
    for m, ref in enumerate(unit_refs):
        ref[...] = normed(x_ref[m, 0].astype(F32), gain_ref[0:1, :])


def load_body(*refs):
    sems, refs = refs[-1], refs[:-1]
    count = len(refs) // 2
    copies = []
    for ref, into in zip(refs[:count], refs[count:]):
        rows = ref.shape[1] // 4
        for b in range(ref.shape[0]):
            for i in range(4):
                part = pl.ds(i * rows, rows)
                copies.append(
                    pltpu.make_async_copy(ref.at[b, part], into.at[b, part], sems.at[len(copies)])
                )
    for copy in copies:
        copy.start()
    for copy in copies:
        copy.wait()


def block_body(b, member, odd_ref, x_ref, near_ref, mid_ref, far_ref, conv_ref, up_ref, down_ref, *rest):
    last = b == BLOCKS - 1
    *rest, mixed = rest
    if last and member == 0:
        cell_ref, chan_ref, out_ref, seen_ref, fields_ref = rest
    elif last:
        cell_ref, chan_ref, first_ref, seen_ref, out_ref, all_seen_ref, fields_ref = rest
    else:
        gain_ref, fields_ref, unit_ref = rest
    lon, ch = x_ref.shape
    rows = jnp.concatenate([near_ref[...], mid_ref[...], far_ref[...]], axis=1)
    lines = (2 - 2 * odd_ref[0], 1, 2 * odd_ref[0])
    parts = []
    for q in range(3):
        taps = [
            conv_ref[b, pl.ds(pl.multiple_of((p * 3 + q) * ch, ch), ch), :] for p in lines
        ]
        parts.append(jnp.dot(rows, jnp.concatenate(taps, axis=0), preferred_element_type=F32))
    mixed[...] = (
        pltpu.roll(parts[0], 1, 0) + parts[1] + pltpu.roll(parts[2], lon - 1, 0)
    ).astype(BF16)
    step = 144
    for start in range(0, lon, step):
        part = pl.ds(start, step)
        hidden = jax.nn.gelu(jnp.dot(mixed[part, :], up_ref[b], preferred_element_type=F32))
        branch = jnp.dot(hidden.astype(BF16), down_ref[b], preferred_element_type=F32)
        fields = (x_ref[part, :].astype(F32) + branch).astype(BF16)
        fields_ref[part, :] = fields
        if not last:
            unit_ref[part, :] = normed(fields.astype(F32), gain_ref[b + 1 : b + 2, :])
    if last:
        owners = out_ref.shape[0]
        cells = fields_ref.shape[0] // owners
        count = cell_ref.shape[1]
        at_cell = lax.broadcasted_iota(jnp.int32, (lon, count), 0) == cell_ref[...]
        pick = jnp.where(at_cell, 1.0, 0.0).astype(BF16)
        column = lax.dot_general(
            fields_ref[:lon, :], pick, (((0,), (0,)), ((), ())), preferred_element_type=F32
        )
        at_chan = lax.broadcasted_iota(jnp.int32, (ch, count), 0) == chan_ref[...]
        seen = jnp.sum(jnp.where(at_chan, column, 0.0), axis=0, keepdims=True)
        seen = [seen[:, i : i + ch] for i in range(0, count, ch)]
        fields_ref[lon:, :] = jnp.zeros((owners * cells - lon, ch), BF16)
        for i in range(owners):
            out_ref[i, member * cells : (member + 1) * cells, :] = fields_ref[
                i * cells : (i + 1) * cells, :
            ]
        if member == 0:
            seen_ref[...] = jnp.concatenate(seen, axis=0)
        else:
            both = jnp.concatenate([seen_ref[...], *seen], axis=0).astype(BF16)
            for i in range(owners):
                out_ref[i, :cells, :] = first_ref[i]
                all_seen_ref[i] = both


def gram_body(seen_ref, value_ref, var_ref, out_ref):
    owners, _, ch = seen_ref.shape
    lines = value_ref.shape[0]
    seen = seen_ref[...].astype(F32)
    members = 2 * owners
    twice = lambda ref: jnp.concatenate([ref[...], ref[...]], axis=0)
    half = jnp.sum(seen, axis=0)
    centre = (half + pltpu.roll(half, lines, 0)) / members
    anomaly = seen - centre[None]
    scaled = anomaly / twice(var_ref)[None]
    rows = owners * 8
    right = jnp.concatenate([anomaly.reshape(rows, ch), twice(value_ref) - centre], axis=0)
    terms = lax.dot_general(
        scaled.reshape(rows, ch),
        right,
        (((1,), (1,)), ((), ())),
        precision=HIGHEST,
        preferred_element_type=F32,
    )
    row = lax.broadcasted_iota(jnp.int32, terms.shape, 0)
    col = lax.broadcasted_iota(jnp.int32, terms.shape, 1)
    terms = jnp.where((row % lines == col % lines) & (col < rows + lines), terms, 0.0)
    dot = functools.partial(jnp.dot, precision=HIGHEST, preferred_element_type=F32)
    left = jnp.where(
        lax.broadcasted_iota(jnp.int32, (members, rows), 0)
        == lax.broadcasted_iota(jnp.int32, (members, rows), 1) // lines,
        1.0,
        0.0,
    )
    gather = jnp.where(
        lax.broadcasted_iota(jnp.int32, (rows + 8, 128), 0) // lines
        == lax.broadcasted_iota(jnp.int32, (rows + 8, 128), 1),
        1.0,
        0.0,
    )
    out_ref[...] = dot(dot(left, terms), gather)


def transform_body(a_ref, b_ref, c_ref, d_ref, out_ref):
    total = (a_ref[...] + b_ref[...]) + (c_ref[...] + d_ref[...])
    members = total.shape[0]
    dot = functools.partial(jnp.dot, precision=HIGHEST, preferred_element_type=F32)
    row = lax.broadcasted_iota(jnp.int32, (members, members), 0)
    col = lax.broadcasted_iota(jnp.int32, (members, members), 1)
    identity = jnp.where(row == col, 1.0, 0.0)
    spread = float(members - 1)
    gram = total[:, :members]
    bound_value = spread + jnp.sum(gram * identity)
    iterate = (spread * identity + gram) / bound_value
    inv_root = identity
    for _ in range(NS_ITERS):
        step_mat = 1.5 * identity - 0.5 * dot(inv_root, iterate)
        iterate = dot(iterate, step_mat)
        inv_root = dot(step_mat, inv_root)
    inv_sqrt = inv_root / jnp.sqrt(bound_value)
    shift = dot(inv_sqrt, dot(inv_sqrt, total))[:, members : members + 1]
    weights = math.sqrt(spread) * inv_sqrt + shift
    totals = jnp.sum(weights, axis=0, keepdims=True)
    out_ref[...] = (weights + (1.0 - totals) / members).astype(BF16)


def combine_body(weight_ref, share_ref, out_ref):
    members = weight_ref.shape[0]
    owners = share_ref.shape[0]
    cells = out_ref.shape[1]
    group = 16
    rows = members * group
    spread = jnp.where(
        lax.broadcasted_iota(jnp.int32, (rows, members), 0) // group
        == lax.broadcasted_iota(jnp.int32, (rows, members), 1),
        1.0,
        0.0,
    ).astype(BF16)
    tall = lax.dot_general(
        spread, weight_ref[...], (((1,), (1,)), ((), ())), preferred_element_type=F32
    ).astype(BF16)
    wide = lax.dot_general(tall, spread, (((1,), (1,)), ((), ())), preferred_element_type=F32)
    same = (
        lax.broadcasted_iota(jnp.int32, (rows, rows), 0) % group
        == lax.broadcasted_iota(jnp.int32, (rows, rows), 1) % group
    )
    kron = jnp.where(same, wide, 0.0).astype(BF16)
    for start in range(0, cells, group):
        part = pl.ds(start, group)
        data = jnp.concatenate(
            [share_ref[i, pl.ds(m * cells + start, group), :] for i in range(owners) for m in range(2)],
            axis=0,
        )
        sums = jnp.dot(kron, data, preferred_element_type=F32).astype(BF16)
        for i in range(members):
            out_ref[i, part, :] = sums[i * group : (i + 1) * group, :]


def place_body(in_ref, out_ref):
    lon = out_ref.shape[2]
    cells = in_ref.shape[2]
    for i in range(lon // cells):
        for m in range(out_ref.shape[0]):
            out_ref[m, 0, i * cells : (i + 1) * cells, :] = in_ref[i, m]


def body(latent, gains, conv, up, down, obs_cell, obs_chan, obs_value, obs_var):
    members, _, lon, ch = latent.shape
    count = obs_cell.shape[0]
    lat = lax.axis_size("lat")
    mem = lax.axis_size("mem")
    cell, chan = (v.reshape(1, count) for v in (obs_cell, obs_chan))
    value, var = (v.reshape(count // ch, ch) for v in (obs_value, obs_var))
    held = [pltpu.VMEM((lon, ch), BF16)]
    odd_row = (lax.axis_index("lat") % 2).reshape(1)
    work = 2 * lon * (9 * ch * ch + 2 * ch * up.shape[2])
    row = shaped((lon, ch), BF16)
    cells = -(-lon // (mem * 16)) * 16

    def halo(unit):
        pairs = [[(i, i + 1) for i in range(start, lat - 1, 2)] for start in (0, 1)]
        return [lax.ppermute(unit, "lat", p + [(j, i) for i, j in p]) for p in pairs]

    def block(b, m, x, near, mid, far, extra, outs, x_spec, halo_spec, scratch=()):
        return call(
            functools.partial(block_body, b, m),
            outs,
            (odd_row, x, near, mid, far, *held_weights, *extra),
            [SMEM, x_spec, halo_spec, halo_spec, halo_spec] + [VMEM] * (3 + len(extra)),
            grid=(1,),
            scratch=[*scratch, *held],
            mib=32,
            flops=work,
            nbytes=8 * lon * ch * 2,
        )

    def latent_spec(m):
        return pl.BlockSpec((None, None, lon, ch), lambda i: (m, 0, 0, 0))

    units = call(first_norm, (row,) * members, (latent, gains), nbytes=8 * lon * ch)
    firsts = [(unit, *halo(unit)) for unit in units]
    weights = (conv, up, down)
    held_weights = call(
        load_body,
        tuple(shaped(w.shape, BF16) for w in weights),
        weights,
        [HBM] * 3,
        scratch=[pltpu.SemaphoreType.DMA((24,))],
        mib=50,
        nbytes=sum(2 * w.size for w in weights),
    )
    fields, lasts = [], []
    for m, (unit, near, far) in enumerate(firsts):
        out, unit = block(
            0, m, latent, near, unit, far, (gains,), (row, row), latent_spec(m), VMEM
        )
        fields.append(out)
        lasts.append((unit, *halo(unit)))
    plain = shaped((mem, cells, ch), BF16)
    both = shaped((mem, members * cells, ch), BF16)
    store = [pltpu.VMEM((mem * cells, ch), BF16)]
    fields[0], _ = lax.optimization_barrier((fields[0], lasts[1][0]))
    unit, near, far = lasts[0]
    outs = (plain, shaped((count // ch, ch), F32))
    even, seen = block(1, 0, fields[0], near, unit, far, (cell, chan), outs, VMEM, VMEM, store)
    unit, near, far = lasts[1]
    outs = (both, shaped((mem, 8, ch), BF16))
    share, seen = block(
        1, 1, fields[1], near, unit, far, (cell, chan, even, seen), outs, VMEM, VMEM, store
    )
    seen = lax.all_to_all(seen, "mem", 0, 0, tiled=True)
    share, seen = lax.optimization_barrier((share, seen))
    share = lax.all_to_all(share, "mem", 0, 0, tiled=True)

    def swap(v, axis, steps):
        size = {"lat": lat, "mem": mem}[axis]
        return [v] + [lax.ppermute(v, axis, [(i, i ^ s) for i in range(size)]) for s in steps]

    square = shaped((members * mem, 128), F32)
    terms = call(
        gram_body,
        square,
        (seen, value, var),
    )
    terms = sum(swap(terms, "lat", (1, 2, 3)))
    sums = swap(terms, "lat", (4, 8, 12))
    weights = call(transform_body, shaped((members * mem, members * mem), BF16), sums)
    mixed = call(combine_body, shaped((members * mem, cells, ch), BF16), (weights, share))
    mixed = lax.all_to_all(mixed.reshape(mem, members, cells, ch), "mem", 0, 0, tiled=True)
    return call(place_body, shaped(latent.shape, BF16), (mixed,))


def solution(mesh):
    in_specs = (
        P("mem", "lat", None, None),
        P(),
        P(),
        P(),
        P(),
        P("lat"),
        P("lat"),
        P("lat"),
        P("lat"),
    )
    out_specs = P("mem", "lat", None, None)
    return jax.shard_map(body, mesh=mesh, in_specs=in_specs, out_specs=out_specs, check_vma=False)
```

```python
import functools
import math

import jax
import jax.numpy as jnp
from jax import lax
from jax.experimental import pallas as pl
from jax.experimental.pallas import tpu as pltpu
from jax.sharding import PartitionSpec as P

BLOCKS = 2
NS_ITERS = 6
F32 = jnp.float32
BF16 = jnp.bfloat16
HIGHEST = lax.Precision.HIGHEST
VMEM = pl.BlockSpec(memory_space=pltpu.VMEM)
SMEM = pl.BlockSpec(memory_space=pltpu.SMEM)
HBM = pl.BlockSpec(memory_space=pltpu.HBM)


def call(body, out_shape, args, specs=None, out_specs=None, scratch=(), mib=24, flops=0, nbytes=0, **kw):
    return pl.pallas_call(
        body,
        out_shape=out_shape,
        in_specs=specs or [VMEM] * len(args),
        out_specs=out_specs if out_specs is not None else jax.tree.map(lambda _: VMEM, out_shape),
        scratch_shapes=list(scratch),
        compiler_params=pltpu.CompilerParams(vmem_limit_bytes=mib << 20),
        cost_estimate=pl.CostEstimate(flops=flops, bytes_accessed=nbytes, transcendentals=0),
        **kw,
    )(*args)


def shaped(shape, dtype):
    return jax.ShapeDtypeStruct(shape, dtype)


def normed(wide, gain):
    factor = lax.rsqrt(jnp.mean(wide * wide, axis=-1, keepdims=True) + 1e-06)
    return (wide * factor * gain).astype(BF16)


def open_body(latent_ref, gain_in_ref, *refs):
    *refs, sems = refs
    gain_ref, refs = refs[0], refs[1:]
    members = len(refs) // 2
    copies = [pltpu.make_async_copy(gain_in_ref, gain_ref, sems.at[members])]
    for m in range(members):
        copies.append(pltpu.make_async_copy(latent_ref.at[m, 0], refs[m], sems.at[m]))
    for copy in copies:
        copy.start()
    copies[0].wait()
    for m in range(members):
        copies[m + 1].wait()
        refs[members + m][...] = normed(refs[m][...].astype(F32), gain_ref[0:1, :])


def load_body(b, *refs):
    sems, refs = refs[-1], refs[:-1]
    count = len(refs) // 2
    copies = []
    for ref, into in zip(refs[:count], refs[count:]):
        rows = ref.shape[1] // 4
        for i in range(4):
            part = pl.ds(i * rows, rows)
            copies.append(
                pltpu.make_async_copy(ref.at[b, part], into.at[part], sems.at[len(copies)])
            )
    for copy in copies:
        copy.start()
    for copy in copies:
        copy.wait()


def block_body(b, member, odd_ref, x_ref, near_ref, mid_ref, far_ref, conv_ref, up_ref, down_ref, *rest):
    last = b == BLOCKS - 1
    *rest, mixed = rest
    if last and member == 0:
        cell_ref, chan_ref, out_ref, seen_ref, fields_ref = rest
    elif last:
        cell_ref, chan_ref, first_ref, seen_ref, out_ref, all_seen_ref, fields_ref = rest
    else:
        gain_ref, fields_ref, unit_ref = rest
    lon, ch = x_ref.shape
    rows = jnp.concatenate([near_ref[...], mid_ref[...], far_ref[...]], axis=1)
    lines = (2 - 2 * odd_ref[0], 1, 2 * odd_ref[0])
    parts = []
    for q in range(3):
        taps = [
            conv_ref[pl.ds(pl.multiple_of((p * 3 + q) * ch, ch), ch), :] for p in lines
        ]
        parts.append(jnp.dot(rows, jnp.concatenate(taps, axis=0), preferred_element_type=F32))
    mixed[...] = (
        pltpu.roll(parts[0], 1, 0) + parts[1] + pltpu.roll(parts[2], lon - 1, 0)
    ).astype(BF16)
    step = 144
    for start in range(0, lon, step):
        part = pl.ds(start, step)
        hidden = jax.nn.gelu(jnp.dot(mixed[part, :], up_ref[...], preferred_element_type=F32))
        branch = jnp.dot(hidden.astype(BF16), down_ref[...], preferred_element_type=F32)
        fields = (x_ref[part, :].astype(F32) + branch).astype(BF16)
        fields_ref[part, :] = fields
        if not last:
            unit_ref[part, :] = normed(fields.astype(F32), gain_ref[b + 1 : b + 2, :])
    if last:
        owners = out_ref.shape[0]
        cells = fields_ref.shape[0] // owners
        count = cell_ref.shape[1]
        at_cell = lax.broadcasted_iota(jnp.int32, (lon, count), 0) == cell_ref[...]
        pick = jnp.where(at_cell, 1.0, 0.0).astype(BF16)
        column = lax.dot_general(
            fields_ref[:lon, :], pick, (((0,), (0,)), ((), ())), preferred_element_type=F32
        )
        at_chan = lax.broadcasted_iota(jnp.int32, (ch, count), 0) == chan_ref[...]
        seen = jnp.sum(jnp.where(at_chan, column, 0.0), axis=0, keepdims=True)
        seen = [seen[:, i : i + ch] for i in range(0, count, ch)]
        fields_ref[lon:, :] = jnp.zeros((owners * cells - lon, ch), BF16)
        for i in range(owners):
            out_ref[i, member * cells : (member + 1) * cells, :] = fields_ref[
                i * cells : (i + 1) * cells, :
            ]
        if member == 0:
            seen_ref[...] = jnp.concatenate(seen, axis=0)
        else:
            both = jnp.concatenate([seen_ref[...], *seen], axis=0).astype(BF16)
            for i in range(owners):
                out_ref[i, :cells, :] = first_ref[i]
                all_seen_ref[i] = both


def gram_body(seen_ref, value_ref, var_ref, out_ref):
    owners, _, ch = seen_ref.shape
    lines = value_ref.shape[0]
    seen = seen_ref[...].astype(F32)
    members = 2 * owners
    twice = lambda ref: jnp.concatenate([ref[...], ref[...]], axis=0)
    half = jnp.sum(seen, axis=0)
    centre = (half + pltpu.roll(half, lines, 0)) / members
    anomaly = seen - centre[None]
    scaled = anomaly / twice(var_ref)[None]
    rows = owners * 8
    right = jnp.concatenate([anomaly.reshape(rows, ch), twice(value_ref) - centre], axis=0)
    terms = lax.dot_general(
        scaled.reshape(rows, ch),
        right,
        (((1,), (1,)), ((), ())),
        precision=HIGHEST,
        preferred_element_type=F32,
    )
    row = lax.broadcasted_iota(jnp.int32, terms.shape, 0)
    col = lax.broadcasted_iota(jnp.int32, terms.shape, 1)
    terms = jnp.where((row % lines == col % lines) & (col < rows + lines), terms, 0.0)
    dot = functools.partial(jnp.dot, precision=HIGHEST, preferred_element_type=F32)
    left = jnp.where(
        lax.broadcasted_iota(jnp.int32, (members, rows), 0)
        == lax.broadcasted_iota(jnp.int32, (members, rows), 1) // lines,
        1.0,
        0.0,
    )
    gather = jnp.where(
        lax.broadcasted_iota(jnp.int32, (rows + 8, 128), 0) // lines
        == lax.broadcasted_iota(jnp.int32, (rows + 8, 128), 1),
        1.0,
        0.0,
    )
    out_ref[...] = dot(dot(left, terms), gather)


def transform_body(a_ref, b_ref, c_ref, d_ref, out_ref):
    total = (a_ref[...] + b_ref[...]) + (c_ref[...] + d_ref[...])
    members = total.shape[0]
    dot = functools.partial(jnp.dot, precision=HIGHEST, preferred_element_type=F32)
    row = lax.broadcasted_iota(jnp.int32, (members, members), 0)
    col = lax.broadcasted_iota(jnp.int32, (members, members), 1)
    identity = jnp.where(row == col, 1.0, 0.0)
    spread = float(members - 1)
    gram = total[:, :members]
    bound_value = spread + jnp.sum(gram * identity)
    iterate = (spread * identity + gram) / bound_value
    inv_root = identity
    for _ in range(NS_ITERS):
        step_mat = 1.5 * identity - 0.5 * dot(inv_root, iterate)
        iterate = dot(iterate, step_mat)
        inv_root = dot(step_mat, inv_root)
    inv_sqrt = inv_root / jnp.sqrt(bound_value)
    shift = dot(inv_sqrt, dot(inv_sqrt, total))[:, members : members + 1]
    weights = math.sqrt(spread) * inv_sqrt + shift
    totals = jnp.sum(weights, axis=0, keepdims=True)
    out_ref[...] = (weights + (1.0 - totals) / members).astype(BF16)


def combine_body(weight_ref, share_ref, out_ref):
    members = weight_ref.shape[0]
    owners = share_ref.shape[0]
    cells = out_ref.shape[1]
    group = 16
    rows = members * group
    spread = jnp.where(
        lax.broadcasted_iota(jnp.int32, (rows, members), 0) // group
        == lax.broadcasted_iota(jnp.int32, (rows, members), 1),
        1.0,
        0.0,
    ).astype(BF16)
    tall = lax.dot_general(
        spread, weight_ref[...], (((1,), (1,)), ((), ())), preferred_element_type=F32
    ).astype(BF16)
    wide = lax.dot_general(tall, spread, (((1,), (1,)), ((), ())), preferred_element_type=F32)
    same = (
        lax.broadcasted_iota(jnp.int32, (rows, rows), 0) % group
        == lax.broadcasted_iota(jnp.int32, (rows, rows), 1) % group
    )
    kron = jnp.where(same, wide, 0.0).astype(BF16)
    for start in range(0, cells, group):
        part = pl.ds(start, group)
        data = jnp.concatenate(
            [share_ref[i, pl.ds(m * cells + start, group), :] for i in range(owners) for m in range(2)],
            axis=0,
        )
        sums = jnp.dot(kron, data, preferred_element_type=F32).astype(BF16)
        for i in range(members):
            out_ref[i, part, :] = sums[i * group : (i + 1) * group, :]


def place_body(in_ref, out_ref):
    lon = out_ref.shape[2]
    cells = in_ref.shape[2]
    for i in range(lon // cells):
        for m in range(out_ref.shape[0]):
            out_ref[m, 0, i * cells : (i + 1) * cells, :] = in_ref[i, m]


def body(latent, gains, conv, up, down, obs_cell, obs_chan, obs_value, obs_var):
    members, _, lon, ch = latent.shape
    count = obs_cell.shape[0]
    lat = lax.axis_size("lat")
    mem = lax.axis_size("mem")
    cell, chan = (v.reshape(1, count) for v in (obs_cell, obs_chan))
    value, var = (v.reshape(count // ch, ch) for v in (obs_value, obs_var))
    odd_row = (lax.axis_index("lat") % 2).reshape(1)
    work = 2 * lon * (9 * ch * ch + 2 * ch * up.shape[2])
    row = shaped((lon, ch), BF16)
    cells = -(-lon // (mem * 16)) * 16

    def halo(unit):
        pairs = [[(i, i + 1) for i in range(start, lat - 1, 2)] for start in (0, 1)]
        return [lax.ppermute(unit, "lat", p + [(j, i) for i, j in p]) for p in pairs]

    def block(b, m, x, near, mid, far, held, extra, outs, scratch=()):
        args = (odd_row, x, near, mid, far, *held, *extra)
        return call(
            functools.partial(block_body, b, m),
            outs,
            args,
            [SMEM] + [VMEM] * (len(args) - 1),
            scratch=[*scratch, pltpu.VMEM((lon, ch), BF16)],
            mib=32,
            flops=work,
            nbytes=8 * lon * ch * 2,
        )

    def load(b, weights):
        return call(
            functools.partial(load_body, b),
            tuple(shaped(w.shape[1:], BF16) for w in weights),
            weights,
            [HBM] * 3,
            scratch=[pltpu.SemaphoreType.DMA((12,))],
            mib=48,
            nbytes=sum(w.size for w in weights),
        )

    gains, *rows = call(
        open_body,
        (shaped(gains.shape, F32),) + (row,) * (2 * members),
        (latent, gains),
        [HBM] * 2,
        scratch=[pltpu.SemaphoreType.DMA((members + 1,))],
        mib=52,
        nbytes=8 * lon * ch,
    )
    firsts = [(unit, *halo(unit)) for unit in rows[members:]]
    weights = (conv, up, down)
    held = load(0, weights)
    fields, lasts = [], []
    for m, (unit, near, far) in enumerate(firsts):
        out, unit = block(0, m, rows[m], near, unit, far, held, (gains,), (row, row))
        fields.append(out)
        lasts.append((unit, *halo(unit)))
    weights, _ = lax.optimization_barrier((weights, lasts[1][0]))
    held = load(1, weights)
    plain = shaped((mem, cells, ch), BF16)
    both = shaped((mem, members * cells, ch), BF16)
    store = [pltpu.VMEM((mem * cells, ch), BF16)]
    fields[0], _ = lax.optimization_barrier((fields[0], lasts[1][0]))
    unit, near, far = lasts[0]
    outs = (plain, shaped((count // ch, ch), F32))
    even, seen = block(1, 0, fields[0], near, unit, far, held, (cell, chan), outs, store)
    unit, near, far = lasts[1]
    outs = (both, shaped((mem, 8, ch), BF16))
    share, seen = block(
        1, 1, fields[1], near, unit, far, held, (cell, chan, even, seen), outs, store
    )
    seen = lax.all_to_all(seen, "mem", 0, 0, tiled=True)
    share, seen = lax.optimization_barrier((share, seen))
    share = lax.all_to_all(share, "mem", 0, 0, tiled=True)

    def swap(v, axis, steps):
        size = {"lat": lat, "mem": mem}[axis]
        return [v] + [lax.ppermute(v, axis, [(i, i ^ s) for i in range(size)]) for s in steps]

    square = shaped((members * mem, 128), F32)
    terms = call(
        gram_body,
        square,
        (seen, value, var),
    )
    terms = sum(swap(terms, "lat", (1, 2, 3)))
    sums = swap(terms, "lat", (4, 8, 12))
    weights = call(transform_body, shaped((members * mem, members * mem), BF16), sums)
    mixed = call(combine_body, shaped((members * mem, cells, ch), BF16), (weights, share))
    mixed = lax.all_to_all(mixed.reshape(mem, members, cells, ch), "mem", 0, 0, tiled=True)
    return call(place_body, shaped(latent.shape, BF16), (mixed,))


def solution(mesh):
    in_specs = (
        P("mem", "lat", None, None),
        P(),
        P(),
        P(),
        P(),
        P("lat"),
        P("lat"),
        P("lat"),
        P("lat"),
    )
    out_specs = P("mem", "lat", None, None)
    return jax.shard_map(body, mesh=mesh, in_specs=in_specs, out_specs=out_specs, check_vma=False)
```

```python
import functools
import math

import jax
import jax.numpy as jnp
from jax import lax
from jax.experimental import pallas as pl
from jax.experimental.pallas import tpu as pltpu
from jax.sharding import PartitionSpec as P

BLOCKS = 2
NS_ITERS = 6
F32 = jnp.float32
BF16 = jnp.bfloat16
HIGHEST = lax.Precision.HIGHEST
VMEM = pl.BlockSpec(memory_space=pltpu.VMEM)
SMEM = pl.BlockSpec(memory_space=pltpu.SMEM)
HBM = pl.BlockSpec(memory_space=pltpu.HBM)


def call(body, out_shape, args, specs=None, out_specs=None, scratch=(), mib=24, flops=0, nbytes=0, **kw):
    return pl.pallas_call(
        body,
        out_shape=out_shape,
        in_specs=specs or [VMEM] * len(args),
        out_specs=out_specs if out_specs is not None else jax.tree.map(lambda _: VMEM, out_shape),
        scratch_shapes=list(scratch),
        compiler_params=pltpu.CompilerParams(vmem_limit_bytes=mib << 20),
        cost_estimate=pl.CostEstimate(flops=flops, bytes_accessed=nbytes, transcendentals=0),
        **kw,
    )(*args)


def shaped(shape, dtype):
    return jax.ShapeDtypeStruct(shape, dtype)


def normed(wide, gain):
    factor = lax.rsqrt(jnp.mean(wide * wide, axis=-1, keepdims=True) + 1e-06)
    return (wide * factor * gain).astype(BF16)


def open_body(latent_ref, gain_in_ref, *refs):
    *refs, sems = refs
    gain_ref, refs = refs[0], refs[1:]
    members = len(refs) // 2
    copies = [pltpu.make_async_copy(gain_in_ref, gain_ref, sems.at[members])]
    for m in range(members):
        copies.append(pltpu.make_async_copy(latent_ref.at[m, 0], refs[m], sems.at[m]))
    for copy in copies:
        copy.start()
    copies[0].wait()
    for m in range(members):
        copies[m + 1].wait()
        refs[members + m][...] = normed(refs[m][...].astype(F32), gain_ref[0:1, :])


def load_body(b, *refs):
    sems, refs = refs[-1], refs[:-1]
    count = len(refs) // 2
    copies = []
    for ref, into in zip(refs[:count], refs[count:]):
        rows = ref.shape[1] // 4
        for i in range(4):
            part = pl.ds(i * rows, rows)
            copies.append(
                pltpu.make_async_copy(ref.at[b, part], into.at[part], sems.at[len(copies)])
            )
    for copy in copies:
        copy.start()
    for copy in copies:
        copy.wait()


def block_body(b, member, odd_ref, x_ref, near_ref, mid_ref, far_ref, conv_ref, up_ref, down_ref, *rest):
    last = b == BLOCKS - 1
    *rest, mixed = rest
    if last and member == 0:
        cell_ref, chan_ref, out_ref, seen_ref, fields_ref = rest
    elif last:
        cell_ref, chan_ref, first_ref, seen_ref, out_ref, all_seen_ref, fields_ref = rest
    else:
        gain_ref, fields_ref, unit_ref = rest
    lon, ch = x_ref.shape
    rows = jnp.concatenate([near_ref[...], mid_ref[...], far_ref[...]], axis=1)
    lines = (2 - 2 * odd_ref[0], 1, 2 * odd_ref[0])
    parts = []
    for q in range(3):
        taps = [
            conv_ref[pl.ds(pl.multiple_of((p * 3 + q) * ch, ch), ch), :] for p in lines
        ]
        parts.append(jnp.dot(rows, jnp.concatenate(taps, axis=0), preferred_element_type=F32))
    mixed[...] = (
        pltpu.roll(parts[0], 1, 0) + parts[1] + pltpu.roll(parts[2], lon - 1, 0)
    ).astype(BF16)
    step = 144
    for start in range(0, lon, step):
        part = pl.ds(start, step)
        hidden = jax.nn.gelu(jnp.dot(mixed[part, :], up_ref[...], preferred_element_type=F32))
        branch = jnp.dot(hidden.astype(BF16), down_ref[...], preferred_element_type=F32)
        fields = (x_ref[part, :].astype(F32) + branch).astype(BF16)
        fields_ref[part, :] = fields
        if not last:
            unit_ref[part, :] = normed(fields.astype(F32), gain_ref[b + 1 : b + 2, :])
    if last:
        owners = out_ref.shape[0]
        cells = fields_ref.shape[0] // owners
        count = cell_ref.shape[1]
        at_cell = lax.broadcasted_iota(jnp.int32, (lon, count), 0) == cell_ref[...]
        pick = jnp.where(at_cell, 1.0, 0.0).astype(BF16)
        column = lax.dot_general(
            fields_ref[:lon, :], pick, (((0,), (0,)), ((), ())), preferred_element_type=F32
        )
        at_chan = lax.broadcasted_iota(jnp.int32, (ch, count), 0) == chan_ref[...]
        seen = jnp.sum(jnp.where(at_chan, column, 0.0), axis=0, keepdims=True)
        seen = [seen[:, i : i + ch] for i in range(0, count, ch)]
        fields_ref[lon:, :] = jnp.zeros((owners * cells - lon, ch), BF16)
        for i in range(owners):
            out_ref[i, member * cells : (member + 1) * cells, :] = fields_ref[
                i * cells : (i + 1) * cells, :
            ]
        if member == 0:
            seen_ref[...] = jnp.concatenate(seen, axis=0)
        else:
            both = jnp.concatenate([seen_ref[...], *seen], axis=0).astype(BF16)
            for i in range(owners):
                out_ref[i, :cells, :] = first_ref[i]
                all_seen_ref[i] = both


def gram_body(seen_ref, value_ref, var_ref, out_ref):
    owners, _, ch = seen_ref.shape
    lines = value_ref.shape[0]
    seen = seen_ref[...].astype(F32)
    members = 2 * owners
    twice = lambda ref: jnp.concatenate([ref[...], ref[...]], axis=0)
    half = jnp.sum(seen, axis=0)
    centre = (half + pltpu.roll(half, lines, 0)) / members
    anomaly = seen - centre[None]
    scaled = anomaly / twice(var_ref)[None]
    rows = owners * 8
    right = jnp.concatenate([anomaly.reshape(rows, ch), twice(value_ref) - centre], axis=0)
    terms = lax.dot_general(
        scaled.reshape(rows, ch),
        right,
        (((1,), (1,)), ((), ())),
        precision=HIGHEST,
        preferred_element_type=F32,
    )
    row = lax.broadcasted_iota(jnp.int32, terms.shape, 0)
    col = lax.broadcasted_iota(jnp.int32, terms.shape, 1)
    terms = jnp.where((row % lines == col % lines) & (col < rows + lines), terms, 0.0)
    dot = functools.partial(jnp.dot, precision=HIGHEST, preferred_element_type=F32)
    left = jnp.where(
        lax.broadcasted_iota(jnp.int32, (members, rows), 0)
        == lax.broadcasted_iota(jnp.int32, (members, rows), 1) // lines,
        1.0,
        0.0,
    )
    gather = jnp.where(
        lax.broadcasted_iota(jnp.int32, (rows + 8, 128), 0) // lines
        == lax.broadcasted_iota(jnp.int32, (rows + 8, 128), 1),
        1.0,
        0.0,
    )
    out_ref[...] = dot(dot(left, terms), gather)


def transform_body(a_ref, b_ref, c_ref, d_ref, out_ref):
    total = (a_ref[...] + b_ref[...]) + (c_ref[...] + d_ref[...])
    members = total.shape[0]
    dot = functools.partial(jnp.dot, precision=HIGHEST, preferred_element_type=F32)
    row = lax.broadcasted_iota(jnp.int32, (members, members), 0)
    col = lax.broadcasted_iota(jnp.int32, (members, members), 1)
    identity = jnp.where(row == col, 1.0, 0.0)
    spread = float(members - 1)
    gram = total[:, :members]
    bound_value = spread + jnp.sum(gram * identity)
    iterate = (spread * identity + gram) / bound_value
    inv_root = identity
    for _ in range(NS_ITERS):
        step_mat = 1.5 * identity - 0.5 * dot(inv_root, iterate)
        iterate = dot(iterate, step_mat)
        inv_root = dot(step_mat, inv_root)
    inv_sqrt = inv_root / jnp.sqrt(bound_value)
    shift = dot(inv_sqrt, dot(inv_sqrt, total))[:, members : members + 1]
    weights = math.sqrt(spread) * inv_sqrt + shift
    totals = jnp.sum(weights, axis=0, keepdims=True)
    out_ref[...] = (weights + (1.0 - totals) / members).astype(BF16)


def combine_body(weight_ref, share_ref, out_ref):
    members = weight_ref.shape[0]
    owners = share_ref.shape[0]
    cells = out_ref.shape[1]
    group = 16
    rows = members * group
    spread = jnp.where(
        lax.broadcasted_iota(jnp.int32, (rows, members), 0) // group
        == lax.broadcasted_iota(jnp.int32, (rows, members), 1),
        1.0,
        0.0,
    ).astype(BF16)
    tall = lax.dot_general(
        spread, weight_ref[...], (((1,), (1,)), ((), ())), preferred_element_type=F32
    ).astype(BF16)
    wide = lax.dot_general(tall, spread, (((1,), (1,)), ((), ())), preferred_element_type=F32)
    same = (
        lax.broadcasted_iota(jnp.int32, (rows, rows), 0) % group
        == lax.broadcasted_iota(jnp.int32, (rows, rows), 1) % group
    )
    kron = jnp.where(same, wide, 0.0).astype(BF16)
    for start in range(0, cells, group):
        part = pl.ds(start, group)
        data = jnp.concatenate(
            [share_ref[i, pl.ds(m * cells + start, group), :] for i in range(owners) for m in range(2)],
            axis=0,
        )
        sums = jnp.dot(kron, data, preferred_element_type=F32).astype(BF16)
        for i in range(members):
            out_ref[i, part, :] = sums[i * group : (i + 1) * group, :]


def place_body(in_ref, out_ref, sems):
    lon = out_ref.shape[2]
    cells = in_ref.shape[2]
    copies = []
    for i in range(lon // cells):
        for m in range(out_ref.shape[0]):
            into = out_ref.at[m, 0, pl.ds(i * cells, cells)]
            copies.append(pltpu.make_async_copy(in_ref.at[i, m], into, sems.at[len(copies)]))
    for copy in copies:
        copy.start()
    for copy in copies:
        copy.wait()


def body(latent, gains, conv, up, down, obs_cell, obs_chan, obs_value, obs_var):
    members, _, lon, ch = latent.shape
    count = obs_cell.shape[0]
    lat = lax.axis_size("lat")
    mem = lax.axis_size("mem")
    cell, chan = (v.reshape(1, count) for v in (obs_cell, obs_chan))
    value, var = (v.reshape(count // ch, ch) for v in (obs_value, obs_var))
    odd_row = (lax.axis_index("lat") % 2).reshape(1)
    work = 2 * lon * (9 * ch * ch + 2 * ch * up.shape[2])
    row = shaped((lon, ch), BF16)
    cells = -(-lon // (mem * 16)) * 16

    def halo(unit):
        pairs = [[(i, i + 1) for i in range(start, lat - 1, 2)] for start in (0, 1)]
        return [lax.ppermute(unit, "lat", p + [(j, i) for i, j in p]) for p in pairs]

    def block(b, m, x, near, mid, far, held, extra, outs, scratch=()):
        args = (odd_row, x, near, mid, far, *held, *extra)
        return call(
            functools.partial(block_body, b, m),
            outs,
            args,
            [SMEM] + [VMEM] * (len(args) - 1),
            scratch=[*scratch, pltpu.VMEM((lon, ch), BF16)],
            mib=32,
            flops=work,
            nbytes=8 * lon * ch * 2,
        )

    def load(b, weights):
        return call(
            functools.partial(load_body, b),
            tuple(shaped(w.shape[1:], BF16) for w in weights),
            weights,
            [HBM] * 3,
            scratch=[pltpu.SemaphoreType.DMA((12,))],
            mib=48,
            nbytes=sum(w.size for w in weights),
        )

    gains, *rows = call(
        open_body,
        (shaped(gains.shape, F32),) + (row,) * (2 * members),
        (latent, gains),
        [HBM] * 2,
        scratch=[pltpu.SemaphoreType.DMA((members + 1,))],
        mib=52,
        nbytes=8 * lon * ch,
    )
    firsts = [(unit, *halo(unit)) for unit in rows[members:]]
    weights = (conv, up, down)
    held = load(0, weights)
    fields, lasts = [], []
    for m, (unit, near, far) in enumerate(firsts):
        out, unit = block(0, m, rows[m], near, unit, far, held, (gains,), (row, row))
        fields.append(out)
        lasts.append((unit, *halo(unit)))
    weights, _ = lax.optimization_barrier((weights, lasts[1][0]))
    held = load(1, weights)
    plain = shaped((mem, cells, ch), BF16)
    both = shaped((mem, members * cells, ch), BF16)
    store = [pltpu.VMEM((mem * cells, ch), BF16)]
    fields[0], _ = lax.optimization_barrier((fields[0], lasts[1][0]))
    unit, near, far = lasts[0]
    outs = (plain, shaped((count // ch, ch), F32))
    even, seen = block(1, 0, fields[0], near, unit, far, held, (cell, chan), outs, store)
    unit, near, far = lasts[1]
    outs = (both, shaped((mem, 8, ch), BF16))
    share, seen = block(
        1, 1, fields[1], near, unit, far, held, (cell, chan, even, seen), outs, store
    )
    seen = lax.all_to_all(seen, "mem", 0, 0, tiled=True)
    share, seen = lax.optimization_barrier((share, seen))
    share = lax.all_to_all(share, "mem", 0, 0, tiled=True)

    def swap(v, axis, steps):
        size = {"lat": lat, "mem": mem}[axis]
        return [v] + [lax.ppermute(v, axis, [(i, i ^ s) for i in range(size)]) for s in steps]

    square = shaped((members * mem, 128), F32)
    terms = call(
        gram_body,
        square,
        (seen, value, var),
    )
    terms = sum(swap(terms, "lat", (1, 2, 3)))
    sums = swap(terms, "lat", (4, 8, 12))
    weights = call(transform_body, shaped((members * mem, members * mem), BF16), sums)
    mixed = call(combine_body, shaped((members * mem, cells, ch), BF16), (weights, share))
    mixed = lax.all_to_all(mixed.reshape(mem, members, cells, ch), "mem", 0, 0, tiled=True)
    return call(
        place_body,
        shaped(latent.shape, BF16),
        (mixed,),
        out_specs=HBM,
        scratch=[pltpu.SemaphoreType.DMA((members * mem,))],
    )


def solution(mesh):
    in_specs = (
        P("mem", "lat", None, None),
        P(),
        P(),
        P(),
        P(),
        P("lat"),
        P("lat"),
        P("lat"),
        P("lat"),
    )
    out_specs = P("mem", "lat", None, None)
    return jax.shard_map(body, mesh=mesh, in_specs=in_specs, out_specs=out_specs, check_vma=False)
```
